32 devices in a mesh: groups: 2 (over y), owners: 4 (over z), section: 2 (over x), rep: 2 (over core).
Axes of the slice: x: 2, y: 2, z: 4, core: 2. Of those that a mesh axis runs over, the one named last changes fastest.
Arguments:
- inputs: bfloat16 [2, 4096, 512], P('section', 'owners', ('groups', 'rep')), parts along dimension 2, may hold values from -6 to 6
- weight_first: bfloat16 [2, 32, 2048, 128], P('section', ('owners', 'rep')), may hold values from -0.1875 to 0.1875
- weight_second: bfloat16 [2, 32, 1024, 128], P('section', ('owners', 'rep')), may hold values from -0.25 to 0.25
- bias_first: float32 [2, 4096], P('section', 'owners'), may hold values from -1.5 to 1.5
- bias_second: float32 [2, 4096], P('section', 'owners'), may hold values from -1.5 to 1.5
- links_first: int32 [2, 32, 16], P('section', 'owners'), may hold values from 0 to 15, as said below
- links_second: int32 [2, 32, 8], P('section', 'owners'), may hold values from 0 to 7, as said below
Outputs:
- final_activity: bfloat16 [2, 4096, 512], P('section', 'owners', ('groups', 'rep')), parts along dimension 2
The draws below stay inside these ranges and needn't reach their ends.
There are 2 independent parts, one for each index of `groups`. The reference program is written for one: setup_inputs(seed, part) draws one part's arguments, and reference() takes and returns one part's arrays. A program takes and returns all parts, laid end to end along the dimension named above; an argument that names none is the same for every part. Nothing has to cross between parts.
Inputs may be any that keep to these rules, and one draw needn't show every extreme that they name: `links_first`: in every row of every section the 16 entries are distinct. `links_second`: in every row of every section the 8 entries are distinct.
All inputs are finite; a program needn't handle non-finite values.
Results may differ from the reference program's by a relative error of at most 0.014.
Values may be sent and summed in bfloat16 or wider, within the bound.
A program may use at most 64 MiB of HBM per device.

```python
import jax
import jax.numpy as jnp
from jax import lax

BLOCK = 128
RADIX_A = 16
RADIX_B = 8
NN = 4096
NB = 32
BATCH = 256
MICRO = 2
N_OWNERS = 4
N_SECTION = 2


def draw_links_first(key, part):
    key_list = jax.random.split(jax.random.fold_in(key, 11), N_SECTION * NB)
    shuffled = jax.vmap(lambda subkey: jax.random.permutation(subkey, RADIX_A))(key_list)
    return shuffled.reshape(N_SECTION, NB, RADIX_A).astype(jnp.int32)


def draw_links_second(key, part):
    key_list = jax.random.split(jax.random.fold_in(key, 23), N_SECTION * NB)
    shuffled = jax.vmap(lambda subkey: jax.random.permutation(subkey, RADIX_B))(key_list)
    return shuffled.reshape(N_SECTION, NB, RADIX_B).astype(jnp.int32)


def level_of(own_key, dims, cuts, smallest, high):
    loudness = 1.0
    for dim, parts in cuts:
        draws = jax.random.uniform(jax.random.fold_in(jax.random.fold_in(own_key, 6), dim), (parts,), jnp.float32, smallest / len(cuts), high / len(cuts))
        loudness = loudness * jnp.repeat(jnp.exp(draws), dims[dim] // parts).reshape((-1,) + (1,) * (len(dims) - 1 - dim))
    return loudness


def scatter_about(stream_key, extent, width, limit, cuts=(), kind=jnp.bfloat16):
    array = width * jax.random.normal(stream_key, extent, jnp.float32)
    if cuts:
        array = array * level_of(stream_key, extent, cuts, -0.22, 0.18)
    return jnp.clip(array, -limit, limit).astype(kind)


def setup_inputs(seed: int = 0, part: int = 0) -> dict:
    key_of = jax.random.split(jax.random.key(seed), 8)
    part_splits = jax.random.split(jax.random.fold_in(key_of[7], part), 8)
    inputs = scatter_about(part_splits[0], (MICRO, NN, BATCH), 1.0, 6.0, ((0, 2), (1, 4), (2, 2)))
    weight_first = scatter_about(key_of[1], (N_SECTION, NB, RADIX_A * BLOCK, BLOCK), (RADIX_A * BLOCK // 2) ** -0.5, 0.1875, ((0, 2), (1, 8)))
    weight_second = scatter_about(key_of[2], (N_SECTION, NB, RADIX_B * BLOCK, BLOCK), (RADIX_B * BLOCK // 2) ** -0.5, 0.25, ((0, 2), (1, 8)))
    bias_first = scatter_about(key_of[3], (N_SECTION, NN), 0.3, 1.5, ((0, 2), (1, 4)), jnp.float32)
    bias_second = scatter_about(key_of[4], (N_SECTION, NN), 0.3, 1.5, ((0, 2), (1, 4)), jnp.float32)
    links_first = draw_links_first(jax.random.fold_in(key_of[7], 71), part)
    links_second = draw_links_second(jax.random.fold_in(key_of[7], 71), part)
    return {"inputs": inputs, "weight_first": weight_first, "weight_second": weight_second, "bias_first": bias_first, "bias_second": bias_second, "links_first": links_first, "links_second": links_second}


CEILING = 4.0


def regroup(activity):
    owner_width = activity.shape[0] // N_OWNERS
    piece_len = owner_width // N_OWNERS
    batch_len = activity.shape[1]
    shaped = activity.reshape(N_OWNERS, N_OWNERS, piece_len, batch_len)
    return jnp.transpose(shaped, (1, 0, 2, 3)).reshape(activity.shape)


def radix_layer(activity, tiles, link_table, bias_row):
    radix_len = link_table.shape[1]
    groups_total = link_table.shape[0] // radix_len
    tile_size = tiles.shape[2]
    batch_len = activity.shape[1]
    grouped_act = activity.reshape(groups_total, radix_len, tile_size, batch_len)
    grouped_tiles = tiles.reshape(groups_total, radix_len, radix_len * tile_size, tile_size)
    grouped_links = link_table.reshape(groups_total, radix_len, radix_len)
    grouped_bias = bias_row.reshape(groups_total, radix_len, tile_size)

    def one_group(packed):
        blocks, tile_group, link_group, bias_group = packed
        picked = jnp.take(blocks, link_group, axis=0)
        picked = picked.reshape(radix_len, radix_len * tile_size, batch_len).astype(jnp.float32)
        summed = jnp.einsum("bkc,bkr->bcr", tile_group.astype(jnp.float32), picked,
                            precision=lax.Precision.HIGHEST)
        summed = summed + bias_group[:, :, None]
        return jnp.clip(summed, 0.0, CEILING).astype(jnp.bfloat16)

    mapped = lax.map(one_group, (grouped_act, grouped_tiles, grouped_links, grouped_bias))
    return mapped.reshape(link_table.shape[0] * tile_size, batch_len)


def reference(inputs, weight_first, weight_second, bias_first, bias_second, links_first, links_second):
    results = []
    for micro_idx in range(MICRO):
        activity = inputs[micro_idx]
        for section_pos in range(N_SECTION):
            activity = radix_layer(regroup(activity), weight_first[section_pos], links_first[section_pos], bias_first[section_pos])
            activity = radix_layer(regroup(activity), weight_second[section_pos], links_second[section_pos], bias_second[section_pos])
        results.append(activity)
    return jnp.stack(results)
```

```python
import functools
import math

import jax
import jax.numpy as jnp
from jax import lax
from jax.experimental import pallas as pl
from jax.experimental.pallas import tpu as pltpu
from jax.sharding import PartitionSpec as P

CEILING = 4.0
MESH = pl.DeviceIdType.MESH


def relay(dims, x, w1, w2, b1, b2, l1, l2, o, raw1, far1, raw2, far2, til1, til2, col1, col2,
          in_a, in_b, mid, res, acc, s_w, r_w, l_w, s_in, s_a, r_a, s_b, r_b, s_o, r_o):
    n, sections, span, chunks, tile = dims
    me = lax.axis_index("owners")
    sec = lax.axis_index("section")
    rep = lax.axis_index("rep")
    piece = x.shape[1]
    width = n * piece
    rows = x.shape[2]
    blocks = width // tile
    half = w1.shape[0]
    per = n // chunks
    sub = blocks // chunks
    last = sections - 1

    barrier = pltpu.get_barrier_semaphore()
    for t in range(sections):
        for w in range(n):
            @pl.when(jnp.logical_or(me != w, sec != t))
            def _():
                pl.semaphore_signal(barrier, inc=1, device_id={"owners": w, "section": t}, device_id_type=MESH)
    pl.semaphore_signal(barrier, inc=1, device_id={"rep": 1 - rep}, device_id_type=MESH)

    local = [
        pltpu.make_async_copy(w1, raw1, l_w.at[0]),
        pltpu.make_async_copy(w2, raw2, l_w.at[1]),
    ]
    for copy in local:
        copy.start()
    pl.semaphore_wait(barrier, n * sections)

    def pair_of(w):
        return (w // span) * span

    def send_a(src, m_slot, w, target, send_sem, recv_sem):
        return pltpu.make_async_remote_copy(
            src_ref=src.at[pl.ds(pair_of(w), span)],
            dst_ref=in_a.at[m_slot, :, me],
            send_sem=send_sem, recv_sem=recv_sem,
            device_id={"owners": w, "section": target}, device_id_type=MESH)

    def own_in():
        return pltpu.make_async_copy(x.at[pl.ds(pair_of(me), span)], in_a.at[0, :, me], r_a.at[0, me])

    for d in range(n - 1, -1, -1):
        w = lax.rem(me + d, n)
        if d == 0:
            @pl.when(sec == 0)
            def _():
                own_in().start()

            @pl.when(sec != 0)
            def _():
                send_a(x, sec, w, 0, s_in.at[d], r_a.at[sec, me]).start()
        else:
            send_a(x, sec, w, 0, s_in.at[d], r_a.at[sec, me]).start()

    def weight_copy(src, dst, k):
        return pltpu.make_async_remote_copy(
            src_ref=src, dst_ref=dst,
            send_sem=s_w.at[k], recv_sem=r_w.at[k],
            device_id={"rep": 1 - rep}, device_id_type=MESH)

    weight_copy(w1, far1, 0).start()
    weight_copy(w2, far2, 1).start()

    def arrange(raw, til, links, begin, spans):
        radix = spans * blocks

        def one(b, carry):
            i = b + begin
            taken = [links[i, k] for k in range(radix)]
            for p in range(radix):
                slot = jnp.int32(0)
                for k in range(1, radix):
                    slot = jnp.where(taken[k] == p, k, slot)
                h, j = p // blocks, p % blocks
                c, q = j // sub, h * sub + j % sub
                til[c, pl.ds(pl.multiple_of(i * tile, tile), tile), q * tile:(q + 1) * tile] = raw[b, slot].T
            return carry

        lax.fori_loop(0, half, one, 0)

    def bias_columns(b, col):
        for i in range(blocks):
            row = b[0:1, i * tile:(i + 1) * tile]
            col[i * tile:(i + 1) * tile, :] = jnp.broadcast_to(row, (rows, tile)).T

    bias_columns(b1, col1)
    bias_columns(b2, col2)
    local[0].wait()
    arrange(raw1, til1, l1, rep * half, span)
    weight_copy(w1, far1, 0).wait_recv()
    arrange(far1, til1, l1, (1 - rep) * half, span)

    def finish(col):
        return jnp.clip(acc[...] + col[...], 0.0, CEILING).astype(jnp.bfloat16)

    mine = me // per
    for m in range(sections):
        for d in range(chunks):
            c = lax.rem(mine + d, chunks)
            for k in range(per):
                u = c * per + k
                pltpu.make_async_copy(in_a.at[m, :, u], in_a.at[m, :, u], r_a.at[m, u]).wait()
            v = in_a[m, :, pl.ds(c * per, per)].reshape(span * per * piece, rows)
            part = jnp.dot(til1[c], v, preferred_element_type=jnp.float32)
            acc[...] = part if d == 0 else acc[...] + part
        mid[m] = finish(col1).reshape(n, piece, rows)
        for d in range(n - 1, 0, -1):
            w = lax.rem(me + d, n)
            pltpu.make_async_remote_copy(
                src_ref=mid.at[m, w], dst_ref=in_b.at[m, me],
                send_sem=s_b.at[m, d], recv_sem=r_b.at[m, me],
                device_id={"owners": w}, device_id_type=MESH).start()
        in_b[m, me] = mid[m, me]
        if m == 0:
            local[1].wait()
            arrange(raw2, til2, l2, rep * half, 1)
            weight_copy(w2, far2, 1).wait_recv()
            arrange(far2, til2, l2, (1 - rep) * half, 1)
        for d in range(chunks):
            c = lax.rem(mine + d, chunks)
            for k in range(per):
                u = c * per + k
                if d == 0:
                    @pl.when(u != me)
                    def _():
                        pltpu.make_async_copy(in_b.at[m, u], in_b.at[m, u], r_b.at[m, u]).wait()
                else:
                    pltpu.make_async_copy(in_b.at[m, u], in_b.at[m, u], r_b.at[m, u]).wait()
            v = in_b[m, pl.ds(c * per, per)].reshape(per * piece, rows)
            part = jnp.dot(til2[c], v, preferred_element_type=jnp.float32)
            acc[...] = part if d == 0 else acc[...] + part
        res[m] = finish(col2).reshape(n, piece, rows)

        if last > 0:
            @pl.when(sec < last)
            def _():
                for d in range(n - 1, -1, -1):
                    send_a(res.at[m], m, lax.rem(me + d, n), sec + 1, s_a.at[m, d], r_a.at[m, me]).start()

        @pl.when(sec == last)
        def _():
            if m == last:
                o[...] = res[m]
            else:
                pltpu.make_async_remote_copy(
                    src_ref=res.at[m], dst_ref=o, send_sem=s_o.at[m], recv_sem=r_o.at[0],
                    device_id={"section": m}, device_id_type=MESH).start()

    def sent(ref, sem):
        pltpu.make_async_copy(ref, ref, sem).wait()

    for d in range(n):
        if d == 0:
            @pl.when(sec != 0)
            def _():
                sent(in_a.at[0, :, 0], s_in.at[d])
        else:
            sent(in_a.at[0, :, 0], s_in.at[d])
    for m in range(sections):
        for d in range(1, n):
            sent(mid.at[m, 0], s_b.at[m, d])
    weight_copy(w1, far1, 0).wait_send()
    weight_copy(w2, far2, 1).wait_send()
    if last > 0:
        @pl.when(sec < last)
        def _():
            for m in range(sections):
                for d in range(n):
                    sent(in_a.at[m, :, 0], s_a.at[m, d])
            sent(o, r_o.at[0])

        @pl.when(sec == last)
        def _():
            for m in range(last):
                sent(res.at[m], s_o.at[m])


def body(inputs, weight_first, weight_second, bias_first, bias_second, links_first, links_second):
    n = lax.axis_size("owners")
    sections = lax.axis_size("section")
    width, rows = inputs.shape[1:]
    half, deep, tile = weight_first.shape[1:]
    radix_a = links_first.shape[2]
    radix_b = links_second.shape[2]
    blocks = width // tile
    span = radix_a // blocks
    piece = width // n
    chunks = math.gcd(math.gcd(n, blocks), 4)
    dims = (n, sections, span, chunks, tile)
    bf = jnp.bfloat16
    anyspace = pl.BlockSpec(memory_space=pl.ANY)
    vmem = pl.BlockSpec(memory_space=pltpu.VMEM)
    smem = pl.BlockSpec(memory_space=pltpu.SMEM)
    dma = pltpu.SemaphoreType.DMA
    out = pl.pallas_call(
        functools.partial(relay, dims),
        name="relay",
        out_shape=jax.ShapeDtypeStruct((n, piece, rows), bf),
        in_specs=[anyspace, anyspace, anyspace, vmem, vmem, smem, smem],
        out_specs=vmem,
        scratch_shapes=[
            pltpu.VMEM((half, radix_a, tile, tile), bf),
            pltpu.VMEM((half, radix_a, tile, tile), bf),
            pltpu.VMEM((half, radix_b, tile, tile), bf),
            pltpu.VMEM((half, radix_b, tile, tile), bf),
            pltpu.VMEM((chunks, width, radix_a * tile // chunks), bf),
            pltpu.VMEM((chunks, width, radix_b * tile // chunks), bf),
            pltpu.VMEM((width, rows), jnp.float32),
            pltpu.VMEM((width, rows), jnp.float32),
            pltpu.VMEM((sections, span, n, piece, rows), bf),
            pltpu.VMEM((sections, n, piece, rows), bf),
            pltpu.VMEM((sections, n, piece, rows), bf),
            pltpu.VMEM((sections, n, piece, rows), bf),
            pltpu.VMEM((width, rows), jnp.float32),
            dma((2,)), dma((2,)), dma((2,)),
            dma((n,)), dma((sections, n)), dma((sections, n)),
            dma((sections, n)), dma((sections, n)),
            dma((sections,)), dma((1,)),
        ],
        compiler_params=pltpu.CompilerParams(
            collective_id=0, has_side_effects=True, vmem_limit_bytes=40 * 1024 * 1024),
    )(
        inputs.reshape(n, piece, rows),
        weight_first.reshape(half, radix_a, tile, tile),
        weight_second.reshape(half, radix_b, tile, tile),
        bias_first, bias_second, links_first[0], links_second[0],
    )
    return out.reshape(1, width, rows)


def solution(mesh):
    placed = (
        P("section", "owners", ("groups", "rep")),
        P("section", ("owners", "rep"), None, None),
        P("section", ("owners", "rep"), None, None),
        P("section", "owners"),
        P("section", "owners"),
        P("section", "owners", None),
        P("section", "owners", None),
    )
    return jax.shard_map(
        body,
        mesh=mesh,
        in_specs=placed,
        out_specs=P("section", "owners", ("groups", "rep")),
        check_vma=False,
    )
```

```python
import functools
import math

import jax
import jax.numpy as jnp
from jax import lax
from jax.experimental import pallas as pl
from jax.experimental.pallas import tpu as pltpu
from jax.sharding import PartitionSpec as P

CEILING = 4.0
MESH = pl.DeviceIdType.MESH


def relay(dims, x, w1, w2, b1_in, b2_in, l1_in, l2_in, o, b1, b2, l1, l2, raw1, far1, raw2, far2, til1, til2, col1, col2,
          in_a, in_b, mid, res, acc, s_w, r_w, l_w, s_in, s_a, r_a, s_f, s_b, r_b, s_o, r_o):
    n, sections, span, chunks, tile = dims
    me = lax.axis_index("owners")
    sec = lax.axis_index("section")
    rep = lax.axis_index("rep")
    piece = x.shape[1]
    width = n * piece
    rows = x.shape[2]
    blocks = width // tile
    half = w1.shape[0]
    per = n // chunks
    sub = blocks // chunks
    last = sections - 1

    barrier = pltpu.get_barrier_semaphore()
    for t in range(sections):
        for w in range(n):
            @pl.when(jnp.logical_or(me != w, sec != t))
            def _():
                pl.semaphore_signal(barrier, inc=1, device_id={"owners": w, "section": t}, device_id_type=MESH)
    pl.semaphore_signal(barrier, inc=1, device_id={"rep": 1 - rep}, device_id_type=MESH)

    local = [
        pltpu.make_async_copy(w1, raw1, l_w.at[0]),
        pltpu.make_async_copy(w2, raw2, l_w.at[1]),
        pltpu.make_async_copy(l1_in, l1, l_w.at[2]),
        pltpu.make_async_copy(l2_in, l2, l_w.at[3]),
        pltpu.make_async_copy(b1_in, b1, l_w.at[4]),
        pltpu.make_async_copy(b2_in, b2, l_w.at[5]),
    ]
    for copy in local:
        copy.start()
    pl.semaphore_wait(barrier, n * sections)

    par = lax.rem(me, span)
    base = me - par
    classes = n // span
    bytes_of = in_a.at[0, 0, 0]

    def fellow(k):
        return lax.rem(me + span * k, n)

    def mate(j):
        return base + lax.rem(par + j, span)

    def send_a(src, slot, h, w, target, sem):
        pltpu.make_async_remote_copy(
            src_ref=src.at[(w // span) * span + h], dst_ref=in_a.at[slot, h, me],
            send_sem=sem.at[h, w], recv_sem=r_a.at[slot, h, me],
            device_id={"owners": w, "section": target}, device_id_type=MESH).start()

    def done(sem):
        pltpu.make_async_copy(bytes_of, bytes_of, sem).wait()

    def home_targets():
        return [fellow(k) for k in range(1, classes)] + [mate(j) for j in range(1, span)]

    @pl.when(sec == 0)
    def _():
        for w in home_targets():
            for h in range(span):
                send_a(x, 0, h, w, 0, s_in)
        for h in range(span):
            pltpu.make_async_copy(x.at[base + h], in_a.at[0, h, me], r_a.at[0, h, me]).start()

    @pl.when(sec != 0)
    def _():
        for d in range(n - 1, -1, -1):
            for h in range(span):
                send_a(x, sec + 1, h, lax.rem(me + d, n), 0, s_in)

    def weight_copy(src, dst, k):
        return pltpu.make_async_remote_copy(
            src_ref=src, dst_ref=dst,
            send_sem=s_w.at[k], recv_sem=r_w.at[k],
            device_id={"rep": 1 - rep}, device_id_type=MESH)

    weight_copy(w1, far1, 0).start()
    weight_copy(w2, far2, 1).start()

    def arrange(raw, til, links, begin, spans):
        radix = spans * blocks

        def one(b, carry):
            i = b + begin
            taken = [links[i, k] for k in range(radix)]
            for p in range(radix):
                slot = jnp.int32(0)
                for k in range(1, radix):
                    slot = jnp.where(taken[k] == p, k, slot)
                h, j = p // blocks, p % blocks
                c, q = j // sub, h * sub + j % sub
                til[c, pl.ds(pl.multiple_of(i * tile, tile), tile), q * tile:(q + 1) * tile] = raw[b, slot].T
            return carry

        lax.fori_loop(0, half, one, 0)

    def bias_columns(b, col):
        for i in range(blocks):
            row = b[0:1, i * tile:(i + 1) * tile]
            col[i * tile:(i + 1) * tile, :] = jnp.broadcast_to(row, (rows, tile)).T

    for copy in local[2:]:
        copy.wait()
    bias_columns(b1, col1)
    bias_columns(b2, col2)
    local[0].wait()
    arrange(raw1, til1, l1, rep * half, span)
    weight_copy(w1, far1, 0).wait_recv()
    arrange(far1, til1, l1, (1 - rep) * half, span)

    def finish(col):
        return jnp.clip(acc[...] + col[...], 0.0, CEILING).astype(jnp.bfloat16)

    mine = me // per
    order = sorted(range(chunks), key=lambda d: (d % span, d))

    def slot_of(m):
        return jnp.where(sec == 0, 0, 1) if m == 0 else m + 1

    def forward(m, h, u, j):
        slot = slot_of(m)
        return pltpu.make_async_remote_copy(
            src_ref=in_a.at[slot, h, u], dst_ref=in_a.at[slot, h, u],
            send_sem=s_f.at[m, h, u, j - 1], recv_sem=r_a.at[slot, h, u],
            device_id={"owners": mate(j)}, device_id_type=MESH)

    def forwards(m, act):
        for k in range(classes):
            def go():
                for h in range(span):
                    for j in range(1, span):
                        act(forward(m, h, fellow(k), j))
            if m == 0 and k > 0:
                go()
            else:
                pl.when(sec > 0)(go)

    def first_layer(m):
        slot = slot_of(m)
        for k in range(classes):
            u = fellow(k)
            for h in range(span):
                done(r_a.at[slot, h, u])

                def go():
                    for j in range(1, span):
                        forward(m, h, u, j).start()
                if m == 0 and k > 0:
                    go()
                else:
                    pl.when(sec > 0)(go)
        for e, d in enumerate(order):
            c = lax.rem(mine + d, chunks)
            for k in range(per):
                u = c * per + k

                @pl.when(lax.rem(u, span) != par)
                def _():
                    for h in range(span):
                        done(r_a.at[slot, h, u])
            v = in_a[slot, :, pl.ds(c * per, per)].reshape(span * per * piece, rows)
            part = jnp.dot(til1[c], v, preferred_element_type=jnp.float32)
            acc[...] = part if e == 0 else acc[...] + part
        mid[m] = finish(col1).reshape(n, piece, rows)
        for d in range(n - 1, 0, -1):
            w = lax.rem(me + d, n)
            pltpu.make_async_remote_copy(
                src_ref=mid.at[m, w], dst_ref=in_b.at[m, me],
                send_sem=s_b.at[m, d], recv_sem=r_b.at[m, me],
                device_id={"owners": w}, device_id_type=MESH).start()
        in_b[m, me] = mid[m, me]

    def second_layer(m):
        for d in range(chunks):
            c = lax.rem(mine + d, chunks)
            for k in range(per):
                u = c * per + k
                if d == 0:
                    @pl.when(u != me)
                    def _():
                        done(r_b.at[m, u])
                else:
                    done(r_b.at[m, u])
            v = in_b[m, pl.ds(c * per, per)].reshape(per * piece, rows)
            part = jnp.dot(til2[c], v, preferred_element_type=jnp.float32)
            acc[...] = part if d == 0 else acc[...] + part
        res[m] = finish(col2).reshape(n, piece, rows)

        if last > 0:
            @pl.when(sec < last)
            def _():
                for k in range(classes - 1, -1, -1):
                    for h in range(span):
                        send_a(res.at[m], m + 1, h, fellow(k), sec + 1, s_a.at[m])

        @pl.when(sec == last)
        def _():
            if m == last:
                o[...] = res[m]
            else:
                pltpu.make_async_remote_copy(
                    src_ref=res.at[m], dst_ref=o, send_sem=s_o.at[m], recv_sem=r_o.at[0],
                    device_id={"section": m}, device_id_type=MESH).start()

    first_layer(0)
    local[1].wait()
    arrange(raw2, til2, l2, rep * half, 1)
    weight_copy(w2, far2, 1).wait_recv()
    arrange(far2, til2, l2, (1 - rep) * half, 1)
    for m in range(sections):
        if m < last:
            first_layer(m + 1)
        second_layer(m)

    def sent(ref, sem):
        pltpu.make_async_copy(ref, ref, sem).wait()

    @pl.when(sec == 0)
    def _():
        for w in home_targets():
            for h in range(span):
                done(s_in.at[h, w])

    @pl.when(sec != 0)
    def _():
        for w in range(n):
            for h in range(span):
                done(s_in.at[h, w])
    for m in range(sections):
        forwards(m, lambda copy: copy.wait_send())
        for d in range(1, n):
            sent(mid.at[m, 0], s_b.at[m, d])
    weight_copy(w1, far1, 0).wait_send()
    weight_copy(w2, far2, 1).wait_send()
    if last > 0:
        @pl.when(sec < last)
        def _():
            for m in range(sections):
                for k in range(classes):
                    for h in range(span):
                        done(s_a.at[m, h, fellow(k)])
            sent(o, r_o.at[0])

        @pl.when(sec == last)
        def _():
            for m in range(last):
                sent(res.at[m], s_o.at[m])


def body(inputs, weight_first, weight_second, bias_first, bias_second, links_first, links_second):
    n = lax.axis_size("owners")
    sections = lax.axis_size("section")
    width, rows = inputs.shape[1:]
    half, deep, tile = weight_first.shape[1:]
    radix_a = links_first.shape[2]
    radix_b = links_second.shape[2]
    blocks = width // tile
    span = radix_a // blocks
    piece = width // n
    chunks = math.gcd(math.gcd(n, blocks), 4)
    dims = (n, sections, span, chunks, tile)
    bf = jnp.bfloat16
    anyspace = pl.BlockSpec(memory_space=pltpu.HBM)
    vmem = pl.BlockSpec(memory_space=pltpu.VMEM)
    dma = pltpu.SemaphoreType.DMA
    out = pl.pallas_call(
        functools.partial(relay, dims),
        name="relay",
        out_shape=jax.ShapeDtypeStruct((n, piece, rows), bf),
        in_specs=[anyspace] * 7,
        out_specs=vmem,
        scratch_shapes=[
            pltpu.VMEM(bias_first.shape, jnp.float32),
            pltpu.VMEM(bias_second.shape, jnp.float32),
            pltpu.SMEM(links_first.shape[1:], jnp.int32),
            pltpu.SMEM(links_second.shape[1:], jnp.int32),
            pltpu.VMEM((half, radix_a, tile, tile), bf),
            pltpu.VMEM((half, radix_a, tile, tile), bf),
            pltpu.VMEM((half, radix_b, tile, tile), bf),
            pltpu.VMEM((half, radix_b, tile, tile), bf),
            pltpu.VMEM((chunks, width, radix_a * tile // chunks), bf),
            pltpu.VMEM((chunks, width, radix_b * tile // chunks), bf),
            pltpu.VMEM((width, rows), jnp.float32),
            pltpu.VMEM((width, rows), jnp.float32),
            pltpu.VMEM((sections + 1, span, n, piece, rows), bf),
            pltpu.VMEM((sections, n, piece, rows), bf),
            pltpu.VMEM((sections, n, piece, rows), bf),
            pltpu.VMEM((sections, n, piece, rows), bf),
            pltpu.VMEM((width, rows), jnp.float32),
            dma((2,)), dma((2,)), dma((6,)),
            dma((span, n)), dma((sections, span, n)), dma((sections + 1, span, n)),
            dma((sections, span, n, max(span - 1, 1))),
            dma((sections, n)), dma((sections, n)),
            dma((sections,)), dma((1,)),
        ],
        compiler_params=pltpu.CompilerParams(
            collective_id=0, has_side_effects=True, vmem_limit_bytes=67043328),
    )(
        inputs.reshape(n, piece, rows),
        weight_first.reshape(half, radix_a, tile, tile),
        weight_second.reshape(half, radix_b, tile, tile),
        bias_first, bias_second, links_first[0], links_second[0],
    )
    return out.reshape(1, width, rows)


def solution(mesh):
    placed = (
        P("section", "owners", ("groups", "rep")),
        P("section", ("owners", "rep"), None, None),
        P("section", ("owners", "rep"), None, None),
        P("section", "owners"),
        P("section", "owners"),
        P("section", "owners", None),
        P("section", "owners", None),
    )
    return jax.shard_map(
        body,
        mesh=mesh,
        in_specs=placed,
        out_specs=P("section", "owners", ("groups", "rep")),
        check_vma=False,
    )
```

```python
import functools
import math

import jax
import jax.numpy as jnp
from jax import lax
from jax.experimental import pallas as pl
from jax.experimental.pallas import tpu as pltpu
from jax.sharding import PartitionSpec as P

CEILING = 4.0
MESH = pl.DeviceIdType.MESH


def relay(dims, x, w1, w2, b1_in, b2_in, l1_in, l2_in, o, b1, b2, l1, l2, raw1, far1, raw2, far2, til1, til2, col1, col2,
          in_a, in_b, mid, res, acc, s_w, r_w, l_w, s_in, s_a, r_a, s_f, s_b, r_b, s_o, r_o, ready):
    n, sections, span, chunks, tile = dims
    me = lax.axis_index("owners")
    sec = lax.axis_index("section")
    rep = lax.axis_index("rep")
    piece = x.shape[1]
    width = n * piece
    rows = x.shape[2]
    blocks = width // tile
    half = w1.shape[0]
    per = n // chunks
    sub = blocks // chunks
    last = sections - 1

    barrier = pltpu.get_barrier_semaphore()
    par = lax.rem(me, span)
    base = me - par
    classes = n // span

    def fellow(k):
        return lax.rem(me + span * k, n)

    def mate(j):
        return base + lax.rem(par + j, span)

    def greet(sem, w, t):
        pl.semaphore_signal(sem, inc=1, device_id={"owners": w, "section": t}, device_id_type=MESH)

    near = [fellow(k) for k in range(1, classes)] + [mate(j) for j in range(1, span)]

    @pl.when(sec == 0)
    def _():
        for w in near:
            greet(barrier, w, 0)
    for t in range(1, sections):
        for w in range(n):
            @pl.when(jnp.logical_or(me != w, sec != t))
            def _():
                greet(barrier, w, t)
    pl.semaphore_signal(barrier, inc=1, device_id={"rep": 1 - rep}, device_id_type=MESH)

    local = [
        pltpu.make_async_copy(w1, raw1, l_w.at[0]),
        pltpu.make_async_copy(w2, raw2, l_w.at[1]),
        pltpu.make_async_copy(l1_in, l1, l_w.at[2]),
        pltpu.make_async_copy(l2_in, l2, l_w.at[3]),
        pltpu.make_async_copy(b1_in, b1, l_w.at[4]),
        pltpu.make_async_copy(b2_in, b2, l_w.at[5]),
    ]
    for copy in local:
        copy.start()
    @pl.when(sec == 0)
    def _():
        pl.semaphore_wait(barrier, len(near) + 1)

    @pl.when(sec != 0)
    def _():
        pl.semaphore_wait(barrier, n * sections)

    @pl.when(sec == 1)
    def _():
        for k in range(classes):
            greet(ready, fellow(k), 0)

    bytes_of = in_a.at[0, 0, 0]

    def send_a(src, slot, h, w, target, sem):
        pltpu.make_async_remote_copy(
            src_ref=src.at[(w // span) * span + h], dst_ref=in_a.at[slot, h, me],
            send_sem=sem.at[h, w], recv_sem=r_a.at[slot, h, me],
            device_id={"owners": w, "section": target}, device_id_type=MESH).start()

    def done(sem):
        pltpu.make_async_copy(bytes_of, bytes_of, sem).wait()

    @pl.when(sec == 0)
    def _():
        for w in near:
            for h in range(span):
                send_a(x, 0, h, w, 0, s_in)
        for h in range(span):
            pltpu.make_async_copy(x.at[base + h], in_a.at[0, h, me], r_a.at[0, h, me]).start()

    @pl.when(sec != 0)
    def _():
        for d in range(n - 1, -1, -1):
            for h in range(span):
                send_a(x, sec + 1, h, lax.rem(me + d, n), 0, s_in)

    def weight_copy(src, dst, k):
        return pltpu.make_async_remote_copy(
            src_ref=src, dst_ref=dst,
            send_sem=s_w.at[k], recv_sem=r_w.at[k],
            device_id={"rep": 1 - rep}, device_id_type=MESH)

    weight_copy(w1, far1, 0).start()
    weight_copy(w2, far2, 1).start()

    def arrange(raw, til, links, begin, spans):
        radix = spans * blocks

        def one(b, carry):
            i = b + begin
            taken = [links[i, k] for k in range(radix)]
            for p in range(radix):
                slot = jnp.int32(0)
                for k in range(1, radix):
                    slot = jnp.where(taken[k] == p, k, slot)
                h, j = p // blocks, p % blocks
                c, q = j // sub, h * sub + j % sub
                til[c, pl.ds(pl.multiple_of(i * tile, tile), tile), q * tile:(q + 1) * tile] = raw[b, slot].T
            return carry

        lax.fori_loop(0, half, one, 0)

    def bias_columns(b, col):
        for i in range(blocks):
            row = b[0:1, i * tile:(i + 1) * tile]
            col[i * tile:(i + 1) * tile, :] = jnp.broadcast_to(row, (rows, tile)).T

    for copy in local[2:]:
        copy.wait()
    bias_columns(b1, col1)
    bias_columns(b2, col2)
    local[0].wait()
    arrange(raw1, til1, l1, rep * half, span)
    weight_copy(w1, far1, 0).wait_recv()
    arrange(far1, til1, l1, (1 - rep) * half, span)

    def finish(col):
        return jnp.clip(acc[...] + col[...], 0.0, CEILING).astype(jnp.bfloat16)

    mine = me // per
    order = sorted(range(chunks), key=lambda d: (d % span, d))

    def slot_of(m):
        return jnp.where(sec == 0, 0, 1) if m == 0 else m + 1

    def forward(m, h, u, j):
        slot = slot_of(m)
        return pltpu.make_async_remote_copy(
            src_ref=in_a.at[slot, h, u], dst_ref=in_a.at[slot, h, u],
            send_sem=s_f.at[m, h, u, j - 1], recv_sem=r_a.at[slot, h, u],
            device_id={"owners": mate(j)}, device_id_type=MESH)

    def forwards(m, act):
        for k in range(classes):
            def go():
                for h in range(span):
                    for j in range(1, span):
                        act(forward(m, h, fellow(k), j))
            if m == 0 and k > 0:
                go()
            else:
                pl.when(sec > 0)(go)

    def first_layer(m):
        slot = slot_of(m)
        for k in range(classes):
            u = fellow(k)
            for h in range(span):
                done(r_a.at[slot, h, u])

                def go():
                    for j in range(1, span):
                        forward(m, h, u, j).start()
                if m == 0 and k > 0:
                    go()
                else:
                    pl.when(sec > 0)(go)
        for e, d in enumerate(order):
            c = lax.rem(mine + d, chunks)
            for k in range(per):
                u = c * per + k

                @pl.when(lax.rem(u, span) != par)
                def _():
                    for h in range(span):
                        done(r_a.at[slot, h, u])
            v = in_a[slot, :, pl.ds(c * per, per)].reshape(span * per * piece, rows)
            part = jnp.dot(til1[c], v, preferred_element_type=jnp.float32)
            acc[...] = part if e == 0 else acc[...] + part
        mid[m] = finish(col1).reshape(n, piece, rows)
        for d in range(n - 1, 0, -1):
            w = lax.rem(me + d, n)
            pltpu.make_async_remote_copy(
                src_ref=mid.at[m, w], dst_ref=in_b.at[m, me],
                send_sem=s_b.at[m, d], recv_sem=r_b.at[m, me],
                device_id={"owners": w}, device_id_type=MESH).start()
        in_b[m, me] = mid[m, me]

    def second_layer(m):
        for d in range(chunks):
            c = lax.rem(mine + d, chunks)
            for k in range(per):
                u = c * per + k
                if d == 0:
                    @pl.when(u != me)
                    def _():
                        done(r_b.at[m, u])
                else:
                    done(r_b.at[m, u])
            v = in_b[m, pl.ds(c * per, per)].reshape(per * piece, rows)
            part = jnp.dot(til2[c], v, preferred_element_type=jnp.float32)
            acc[...] = part if d == 0 else acc[...] + part
        res[m] = finish(col2).reshape(n, piece, rows)

        if last > 0:
            @pl.when(sec < last)
            def _():
                if m == 0:
                    @pl.when(sec == 0)
                    def _():
                        pl.semaphore_wait(ready, classes)
                for k in range(classes - 1, -1, -1):
                    for h in range(span):
                        send_a(res.at[m], m + 1, h, fellow(k), sec + 1, s_a.at[m])

        @pl.when(sec == last)
        def _():
            if m == last:
                o[...] = res[m]
            else:
                pltpu.make_async_remote_copy(
                    src_ref=res.at[m], dst_ref=o, send_sem=s_o.at[m], recv_sem=r_o.at[0],
                    device_id={"section": m}, device_id_type=MESH).start()

    first_layer(0)
    local[1].wait()
    arrange(raw2, til2, l2, rep * half, 1)
    weight_copy(w2, far2, 1).wait_recv()
    arrange(far2, til2, l2, (1 - rep) * half, 1)
    for m in range(sections):
        if m > 0:
            first_layer(m)
        second_layer(m)

    def sent(ref, sem):
        pltpu.make_async_copy(ref, ref, sem).wait()

    @pl.when(sec == 0)
    def _():
        for w in near:
            for h in range(span):
                done(s_in.at[h, w])

    @pl.when(sec != 0)
    def _():
        for w in range(n):
            for h in range(span):
                done(s_in.at[h, w])
    for m in range(sections):
        forwards(m, lambda copy: copy.wait_send())
        for d in range(1, n):
            sent(mid.at[m, 0], s_b.at[m, d])
    weight_copy(w1, far1, 0).wait_send()
    weight_copy(w2, far2, 1).wait_send()
    if last > 0:
        @pl.when(sec < last)
        def _():
            for m in range(sections):
                for k in range(classes):
                    for h in range(span):
                        done(s_a.at[m, h, fellow(k)])
            sent(o, r_o.at[0])

        @pl.when(sec == last)
        def _():
            for m in range(last):
                sent(res.at[m], s_o.at[m])


def body(inputs, weight_first, weight_second, bias_first, bias_second, links_first, links_second):
    n = lax.axis_size("owners")
    sections = lax.axis_size("section")
    width, rows = inputs.shape[1:]
    half, deep, tile = weight_first.shape[1:]
    radix_a = links_first.shape[2]
    radix_b = links_second.shape[2]
    blocks = width // tile
    span = radix_a // blocks
    piece = width // n
    chunks = math.gcd(math.gcd(n, blocks), 4)
    dims = (n, sections, span, chunks, tile)
    bf = jnp.bfloat16
    anyspace = pl.BlockSpec(memory_space=pltpu.HBM)
    vmem = pl.BlockSpec(memory_space=pltpu.VMEM)
    dma = pltpu.SemaphoreType.DMA
    out = pl.pallas_call(
        functools.partial(relay, dims),
        name="relay",
        out_shape=jax.ShapeDtypeStruct((n, piece, rows), bf),
        in_specs=[anyspace] * 7,
        out_specs=vmem,
        scratch_shapes=[
            pltpu.VMEM(bias_first.shape, jnp.float32),
            pltpu.VMEM(bias_second.shape, jnp.float32),
            pltpu.SMEM(links_first.shape[1:], jnp.int32),
            pltpu.SMEM(links_second.shape[1:], jnp.int32),
            pltpu.VMEM((half, radix_a, tile, tile), bf),
            pltpu.VMEM((half, radix_a, tile, tile), bf),
            pltpu.VMEM((half, radix_b, tile, tile), bf),
            pltpu.VMEM((half, radix_b, tile, tile), bf),
            pltpu.VMEM((chunks, width, radix_a * tile // chunks), bf),
            pltpu.VMEM((chunks, width, radix_b * tile // chunks), bf),
            pltpu.VMEM((width, rows), jnp.float32),
            pltpu.VMEM((width, rows), jnp.float32),
            pltpu.VMEM((sections + 1, span, n, piece, rows), bf),
            pltpu.VMEM((sections, n, piece, rows), bf),
            pltpu.VMEM((sections, n, piece, rows), bf),
            pltpu.VMEM((sections, n, piece, rows), bf),
            pltpu.VMEM((width, rows), jnp.float32),
            dma((2,)), dma((2,)), dma((6,)),
            dma((span, n)), dma((sections, span, n)), dma((sections + 1, span, n)),
            dma((sections, span, n, max(span - 1, 1))),
            dma((sections, n)), dma((sections, n)),
            dma((sections,)), dma((1,)), pltpu.SemaphoreType.REGULAR,
        ],
        compiler_params=pltpu.CompilerParams(
            collective_id=0, has_side_effects=True, vmem_limit_bytes=67043328),
    )(
        inputs.reshape(n, piece, rows),
        weight_first.reshape(half, radix_a, tile, tile),
        weight_second.reshape(half, radix_b, tile, tile),
        bias_first, bias_second, links_first[0], links_second[0],
    )
    return out.reshape(1, width, rows)


def solution(mesh):
    placed = (
        P("section", "owners", ("groups", "rep")),
        P("section", ("owners", "rep"), None, None),
        P("section", ("owners", "rep"), None, None),
        P("section", "owners"),
        P("section", "owners"),
        P("section", "owners", None),
        P("section", "owners", None),
    )
    return jax.shard_map(
        body,
        mesh=mesh,
        in_specs=placed,
        out_specs=P("section", "owners", ("groups", "rep")),
        check_vma=False,
    )
```

```python
import functools
import math

import jax
import jax.numpy as jnp
from jax import lax
from jax.experimental import pallas as pl
from jax.experimental.pallas import tpu as pltpu
from jax.sharding import PartitionSpec as P

CEILING = 4.0
MESH = pl.DeviceIdType.MESH


def relay(dims, x, w1, w2, b1_in, b2_in, l1_in, l2_in, o, b1, b2, l1, l2, raw1, far1, raw2, far2, til1, til2, col1, col2,
          in_a, in_b, mid, res, acc, s_w, r_w, l_w, s_in, s_a, r_a, s_f, s_b, r_b, s_o, r_o, ready):
    n, sections, span, chunks, tile = dims
    me = lax.axis_index("owners")
    sec = lax.axis_index("section")
    rep = lax.axis_index("rep")
    piece = x.shape[1]
    width = n * piece
    rows = x.shape[2]
    blocks = width // tile
    half = w1.shape[0]
    per = n // chunks
    sub = blocks // chunks
    last = sections - 1

    barrier = pltpu.get_barrier_semaphore()
    par = lax.rem(me, span)
    base = me - par
    classes = n // span

    def fellow(k):
        return lax.rem(me + span * k, n)

    def mate(j):
        return base + lax.rem(par + j, span)

    def greet(sem, w, t):
        pl.semaphore_signal(sem, inc=1, device_id={"owners": w, "section": t}, device_id_type=MESH)

    near = [fellow(k) for k in range(1, classes)] + [mate(j) for j in range(1, span)]

    @pl.when(sec == 0)
    def _():
        for w in near:
            greet(barrier, w, 0)
    for t in range(1, sections):
        for w in range(n):
            @pl.when(jnp.logical_or(me != w, sec != t))
            def _():
                greet(barrier, w, t)
    pl.semaphore_signal(barrier, inc=1, device_id={"rep": 1 - rep}, device_id_type=MESH)

    local = [
        pltpu.make_async_copy(w1, raw1, l_w.at[0]),
        pltpu.make_async_copy(w2, raw2, l_w.at[1]),
        pltpu.make_async_copy(l1_in, l1, l_w.at[2]),
        pltpu.make_async_copy(l2_in, l2, l_w.at[3]),
        pltpu.make_async_copy(b1_in, b1, l_w.at[4]),
        pltpu.make_async_copy(b2_in, b2, l_w.at[5]),
    ]
    for copy in local:
        copy.start()
    @pl.when(sec == 0)
    def _():
        pl.semaphore_wait(barrier, len(near) + 1)

    @pl.when(sec != 0)
    def _():
        pl.semaphore_wait(barrier, n * sections)

    @pl.when(sec == 1)
    def _():
        for k in range(classes):
            greet(ready, fellow(k), 0)

    bytes_of = in_a.at[0, 0, 0]

    def send_a(src, slot, h, w, target, sem):
        pltpu.make_async_remote_copy(
            src_ref=src.at[(w // span) * span + h], dst_ref=in_a.at[slot, h, me],
            send_sem=sem.at[h, w], recv_sem=r_a.at[slot, h, me],
            device_id={"owners": w, "section": target}, device_id_type=MESH).start()

    def done(sem):
        pltpu.make_async_copy(bytes_of, bytes_of, sem).wait()

    @pl.when(sec == 0)
    def _():
        for w in near:
            for h in range(span):
                send_a(x, 0, h, w, 0, s_in)
        for h in range(span):
            pltpu.make_async_copy(x.at[base + h], in_a.at[0, h, me], r_a.at[0, h, me]).start()

    @pl.when(sec != 0)
    def _():
        for d in range(n - 1, -1, -1):
            for h in range(span):
                send_a(x, sec + 1, h, lax.rem(me + d, n), 0, s_in)

    def weight_copy(src, dst, k):
        return pltpu.make_async_remote_copy(
            src_ref=src, dst_ref=dst,
            send_sem=s_w.at[k], recv_sem=r_w.at[k],
            device_id={"rep": 1 - rep}, device_id_type=MESH)

    weight_copy(w1, far1, 0).start()
    weight_copy(w2, far2, 1).start()

    def arrange(raw, til, links, begin, spans):
        radix = spans * blocks

        def one(b, carry):
            i = b + begin
            taken = [links[i, k] for k in range(radix)]
            for p in range(radix):
                slot = jnp.int32(0)
                for k in range(1, radix):
                    slot = jnp.where(taken[k] == p, k, slot)
                h, j = p // blocks, p % blocks
                c, q = j // sub, h * sub + j % sub
                til[c, pl.ds(pl.multiple_of(i * tile, tile), tile), q * tile:(q + 1) * tile] = raw[b, slot].T
            return carry

        lax.fori_loop(0, half, one, 0)

    def bias_columns(b, col):
        for i in range(blocks):
            row = b[0:1, i * tile:(i + 1) * tile]
            col[i * tile:(i + 1) * tile, :] = jnp.broadcast_to(row, (rows, tile)).T

    for copy in local[2:]:
        copy.wait()
    bias_columns(b1, col1)
    bias_columns(b2, col2)
    local[0].wait()
    arrange(raw1, til1, l1, rep * half, span)
    weight_copy(w1, far1, 0).wait_recv()
    arrange(far1, til1, l1, (1 - rep) * half, span)

    def finish(col):
        return jnp.clip(acc[...] + col[...], 0.0, CEILING).astype(jnp.bfloat16)

    mine = me // per
    order = sorted(range(chunks), key=lambda d: (d % span, d))

    def slot_of(m):
        return jnp.where(sec == 0, 0, 1) if m == 0 else m + 1

    def forward(m, h, u, j):
        slot = slot_of(m)
        return pltpu.make_async_remote_copy(
            src_ref=in_a.at[slot, h, u], dst_ref=in_a.at[slot, h, u],
            send_sem=s_f.at[m, h, u, j - 1], recv_sem=r_a.at[slot, h, u],
            device_id={"owners": mate(j)}, device_id_type=MESH)

    def forwards(m, act):
        for k in range(classes):
            def go():
                for h in range(span):
                    for j in range(1, span):
                        act(forward(m, h, fellow(k), j))
            if m == last:
                if m == 0 and k > 0:
                    pl.when(sec == 0)(go)
            elif m == 0 and k > 0:
                go()
            else:
                pl.when(sec > 0)(go)

    def first_layer(m):
        slot = slot_of(m)
        for k in range(classes):
            u = fellow(k)
            for h in range(span):
                done(r_a.at[slot, h, u])

                def go():
                    for j in range(1, span):
                        forward(m, h, u, j).start()
                if m == last:
                    if m == 0 and k > 0:
                        pl.when(sec == 0)(go)
                elif m == 0 and k > 0:
                    go()
                else:
                    pl.when(sec > 0)(go)
        for e, d in enumerate(order):
            c = lax.rem(mine + d, chunks)
            for k in range(per):
                u = c * per + k

                @pl.when(lax.rem(u, span) != par)
                def _():
                    for h in range(span):
                        done(r_a.at[slot, h, u])
            v = in_a[slot, :, pl.ds(c * per, per)].reshape(span * per * piece, rows)
            part = jnp.dot(til1[c], v, preferred_element_type=jnp.float32)
            acc[...] = part if e == 0 else acc[...] + part
        mid[m] = finish(col1).reshape(n, piece, rows)
        for d in range(n - 1, 0, -1):
            w = lax.rem(me + d, n)
            pltpu.make_async_remote_copy(
                src_ref=mid.at[m, w], dst_ref=in_b.at[m, me],
                send_sem=s_b.at[m, d], recv_sem=r_b.at[m, me],
                device_id={"owners": w}, device_id_type=MESH).start()
        in_b[m, me] = mid[m, me]

    def second_layer(m):
        for d in range(chunks):
            c = lax.rem(mine + d, chunks)
            for k in range(per):
                u = c * per + k
                if d == 0:
                    @pl.when(u != me)
                    def _():
                        done(r_b.at[m, u])
                else:
                    done(r_b.at[m, u])
            v = in_b[m, pl.ds(c * per, per)].reshape(per * piece, rows)
            part = jnp.dot(til2[c], v, preferred_element_type=jnp.float32)
            acc[...] = part if d == 0 else acc[...] + part
        res[m] = finish(col2).reshape(n, piece, rows)

        if last > 0:
            @pl.when(sec < last)
            def _():
                if m == 0:
                    @pl.when(sec == 0)
                    def _():
                        pl.semaphore_wait(ready, classes)
                for d in (range(n - 1, -1, -1) if m == last else range(n - span, -1, -span)):
                    for h in range(span):
                        send_a(res.at[m], m + 1, h, lax.rem(me + d, n), sec + 1, s_a.at[m])

        @pl.when(sec == last)
        def _():
            if m == last:
                o[...] = res[m]
            else:
                pltpu.make_async_remote_copy(
                    src_ref=res.at[m], dst_ref=o, send_sem=s_o.at[m], recv_sem=r_o.at[0],
                    device_id={"section": m}, device_id_type=MESH).start()

    first_layer(0)
    local[1].wait()
    arrange(raw2, til2, l2, rep * half, 1)
    weight_copy(w2, far2, 1).wait_recv()
    arrange(far2, til2, l2, (1 - rep) * half, 1)
    for m in range(sections):
        if m > 0:
            first_layer(m)
        second_layer(m)

    def sent(ref, sem):
        pltpu.make_async_copy(ref, ref, sem).wait()

    @pl.when(sec == 0)
    def _():
        for w in near:
            for h in range(span):
                done(s_in.at[h, w])

    @pl.when(sec != 0)
    def _():
        for w in range(n):
            for h in range(span):
                done(s_in.at[h, w])
    for m in range(sections):
        forwards(m, lambda copy: copy.wait_send())
        for d in range(1, n):
            sent(mid.at[m, 0], s_b.at[m, d])
    weight_copy(w1, far1, 0).wait_send()
    weight_copy(w2, far2, 1).wait_send()
    if last > 0:
        @pl.when(sec < last)
        def _():
            for m in range(sections):
                for d in range(0, n, 1 if m == last else span):
                    for h in range(span):
                        done(s_a.at[m, h, lax.rem(me + d, n)])
            sent(o, r_o.at[0])

        @pl.when(sec == last)
        def _():
            for m in range(last):
                sent(res.at[m], s_o.at[m])


def body(inputs, weight_first, weight_second, bias_first, bias_second, links_first, links_second):
    n = lax.axis_size("owners")
    sections = lax.axis_size("section")
    width, rows = inputs.shape[1:]
    half, deep, tile = weight_first.shape[1:]
    radix_a = links_first.shape[2]
    radix_b = links_second.shape[2]
    blocks = width // tile
    span = radix_a // blocks
    piece = width // n
    chunks = math.gcd(math.gcd(n, blocks), 4)
    dims = (n, sections, span, chunks, tile)
    bf = jnp.bfloat16
    anyspace = pl.BlockSpec(memory_space=pltpu.HBM)
    vmem = pl.BlockSpec(memory_space=pltpu.VMEM)
    dma = pltpu.SemaphoreType.DMA
    out = pl.pallas_call(
        functools.partial(relay, dims),
        name="relay",
        out_shape=jax.ShapeDtypeStruct((n, piece, rows), bf),
        in_specs=[anyspace] * 7,
        out_specs=vmem,
        scratch_shapes=[
            pltpu.VMEM(bias_first.shape, jnp.float32),
            pltpu.VMEM(bias_second.shape, jnp.float32),
            pltpu.SMEM(links_first.shape[1:], jnp.int32),
            pltpu.SMEM(links_second.shape[1:], jnp.int32),
            pltpu.VMEM((half, radix_a, tile, tile), bf),
            pltpu.VMEM((half, radix_a, tile, tile), bf),
            pltpu.VMEM((half, radix_b, tile, tile), bf),
            pltpu.VMEM((half, radix_b, tile, tile), bf),
            pltpu.VMEM((chunks, width, radix_a * tile // chunks), bf),
            pltpu.VMEM((chunks, width, radix_b * tile // chunks), bf),
            pltpu.VMEM((width, rows), jnp.float32),
            pltpu.VMEM((width, rows), jnp.float32),
            pltpu.VMEM((sections + 1, span, n, piece, rows), bf),
            pltpu.VMEM((sections, n, piece, rows), bf),
            pltpu.VMEM((sections, n, piece, rows), bf),
            pltpu.VMEM((sections, n, piece, rows), bf),
            pltpu.VMEM((width, rows), jnp.float32),
            dma((2,)), dma((2,)), dma((6,)),
            dma((span, n)), dma((sections, span, n)), dma((sections + 1, span, n)),
            dma((sections, span, n, max(span - 1, 1))),
            dma((sections, n)), dma((sections, n)),
            dma((sections,)), dma((1,)), pltpu.SemaphoreType.REGULAR,
        ],
        compiler_params=pltpu.CompilerParams(
            collective_id=0, has_side_effects=True, vmem_limit_bytes=67043328),
    )(
        inputs.reshape(n, piece, rows),
        weight_first.reshape(half, radix_a, tile, tile),
        weight_second.reshape(half, radix_b, tile, tile),
        bias_first, bias_second, links_first[0], links_second[0],
    )
    return out.reshape(1, width, rows)


def solution(mesh):
    placed = (
        P("section", "owners", ("groups", "rep")),
        P("section", ("owners", "rep"), None, None),
        P("section", ("owners", "rep"), None, None),
        P("section", "owners"),
        P("section", "owners"),
        P("section", "owners", None),
        P("section", "owners", None),
    )
    return jax.shard_map(
        body,
        mesh=mesh,
        in_specs=placed,
        out_specs=P("section", "owners", ("groups", "rep")),
        check_vma=False,
    )
```
